512 devices in a mesh: gx: 16 (over x, y_lo, core), gy: 4 (over y_hi), gz: 8 (over z).
Axes of the slice: x: 4, y: 8 (y_hi: 4, y_lo: 2; y = y_hi * 2 + y_lo), z: 8, core: 2. Of those that a mesh axis runs over, the one named last changes fastest.
Arguments:
- stress_in: float32 [6, 128, 32, 1024], P(None, 'gx', 'gy', 'gz'), may hold values from -6 to 6
- velocity_in: float32 [3, 128, 32, 1024], P(None, 'gx', 'gy', 'gz'), may hold values from -6 to 6
- lame_lambda: float32 [128, 32, 1024], P('gx', 'gy', 'gz'), may hold values from 0.5 to 2
- shear_modulus: float32 [128, 32, 1024], P('gx', 'gy', 'gz'), may hold values from 0.5 to 2
- buoyancy: float32 [128, 32, 1024], P('gx', 'gy', 'gz'), may hold values from 0.5 to 2
- yield_flags: int32 [128, 32, 1024], P('gx', 'gy', 'gz'), may hold values 0 or 1
- panel_cell: int32 [65536], P(('gx', 'gy', 'gz')), may hold values from 0 to 8191, as said below
- panel_normal: float32 [3, 65536], P(None, ('gx', 'gy', 'gz')), may hold values from -4 to 4
- near_block: float32 [65536, 128], P(('gx', 'gy', 'gz')), may hold values from -0.5 to 0.5
- far_rows: float32 [65536, 256], P(('gx', 'gy', 'gz')), may hold values from -0.375 to 0.375
- far_basis: float32 [4096, 65536], P(('gx', 'gy', 'gz')), may hold values from -0.125 to 0.125
- block_ranks: int32 [512, 32], P(('gx', 'gy', 'gz')), may hold values from 2 to 8
Outputs:
- stress_out: float32 [6, 128, 32, 1024], P(None, 'gx', 'gy', 'gz')
- velocity_out: float32 [3, 128, 32, 1024], P(None, 'gx', 'gy', 'gz')
- displacement: float32 [3, 65536], P(None, ('gx', 'gy', 'gz'))
The draws below stay inside these ranges and needn't reach their ends.
Inputs may be any that keep to these rules, and one draw needn't show every extreme that they name: `panel_cell`: a flat index into the owning device's block of 8 x 8 x 128 zones.
All inputs are finite; a program needn't handle non-finite values. No bound on the sum of `yield_flags` on one device may be relied on, other than what follows from the above.
Results may differ from the reference program's by a relative error of at most 0.000073.
Values sent between devices are 32-bit elements; how exact they have to be, the bound alone decides.
No kernel may reach another device: no remote copies, remote signals or barrier semaphores. Data moves between devices by JAX's collectives and lax.ppermute only.
A program may use at most 64 MiB of HBM per device.

```python
import math
import jax
import jax.numpy as jnp
from jax import lax

CX = 8
CY = 8
CZ = 128
SUB = 2
PAN_DEV = 128
RANK = 8
CLUST = 32
BLOCKS = 512
NX = 128
NY = 32
NZ = 1024
PANELS = 65536
N_GX = 16
N_GY = 4
N_GZ = 8


def draw_panel_cell(key, part):
    zones = CX * CY * CZ
    picked = jax.random.randint(key, (PANELS,), 0, zones, dtype=jnp.int32)
    picked = picked.at[0].set(zones - 1)
    picked = picked.at[1].set(0)
    return picked


def touch_ends(result, key, least, largest):
    spot = [jax.random.randint(jax.random.fold_in(key, axis), (), 0, length) for axis, length in enumerate(result.shape)]
    widest = result.shape.index(max(result.shape))
    beside = spot[:widest] + [(spot[widest] + 1) % result.shape[widest]] + spot[widest + 1:]
    return result.at[tuple(spot)].set(least).at[tuple(beside)].set(largest)


def level_of(stream_key, dims, pieces, low, largest):
    level = 1.0
    for position, parts in pieces:
        heights = jax.random.uniform(jax.random.fold_in(jax.random.fold_in(stream_key, 6), position), (parts,), jnp.float32, low / len(pieces), largest / len(pieces))
        level = level * jnp.repeat(jnp.exp(heights), dims[position] // parts).reshape((-1,) + (1,) * (len(dims) - 1 - position))
    return level


def centred(key, dims, width, most, split=(), kind=jnp.bfloat16):
    gain = level_of(key, dims, split, -0.22, 0.18) if split else 1.0
    entries = jax.random.normal(key, dims, jnp.float32) * width * gain
    return jnp.minimum(jnp.maximum(entries, -most), most).astype(kind)


def setup_inputs(seed: int = 0) -> dict:
    key_of = jax.random.split(jax.random.key(seed), 13)
    stress_in = centred(key_of[0], (6, NX, NY, NZ), 1.0, 6.0, ((1, 16), (2, 4), (3, 8)), jnp.float32)
    velocity_in = centred(key_of[1], (3, NX, NY, NZ), 1.0, 6.0, ((1, 16), (2, 4), (3, 8)), jnp.float32)
    lame_lambda = jnp.clip(jnp.exp(math.log(2.0) - 1.3862944 * jax.random.uniform(key_of[2], (NX, NY, NZ), jnp.float32) ** level_of(key_of[2], (NX, NY, NZ), ((0, 16), (1, 4), (2, 8)), -0.2, 0.2)), 0.5, 2.0)
    shear_modulus = jnp.clip(jnp.exp(math.log(2.0) - 1.3862944 * jax.random.uniform(key_of[3], (NX, NY, NZ), jnp.float32) ** level_of(key_of[3], (NX, NY, NZ), ((0, 16), (1, 4), (2, 8)), -0.2, 0.2)), 0.5, 2.0)
    buoyancy = jnp.clip(jnp.exp(math.log(2.0) - 1.3862944 * jax.random.uniform(key_of[4], (NX, NY, NZ), jnp.float32) ** level_of(key_of[4], (NX, NY, NZ), ((0, 16), (1, 4), (2, 8)), -0.2, 0.2)), 0.5, 2.0)
    yield_flags = touch_ends((jax.random.randint(key_of[5], (NX, NY, NZ), 0, 3) < 1).astype(jnp.int32), jax.random.fold_in(key_of[5], 1), 0, 1)
    panel_cell = draw_panel_cell(jax.random.fold_in(key_of[12], 71), 0)
    panel_normal = centred(key_of[7], (3, PANELS), 0.6, 4.0, ((1, 512),), jnp.float32)
    near_block = centred(key_of[8], (PANELS, PAN_DEV), PAN_DEV ** -0.5, 0.5, ((0, 512),), jnp.float32)
    far_rows = centred(key_of[9], (PANELS, CLUST * RANK), (CLUST * RANK) ** -0.5, 0.375, ((0, 512),), jnp.float32)
    far_basis = centred(key_of[10], (RANK * BLOCKS, PANELS), (PANELS // CLUST) ** -0.5, 0.125, ((0, 512),), jnp.float32)
    block_ranks = touch_ends(jax.random.randint(key_of[11], (BLOCKS, CLUST), 2, RANK + 1), jax.random.fold_in(key_of[11], 1), 2, RANK).astype(jnp.int32)
    return dict(stress_in=stress_in, velocity_in=velocity_in, lame_lambda=lame_lambda, shear_modulus=shear_modulus, buoyancy=buoyancy, yield_flags=yield_flags, panel_cell=panel_cell, panel_normal=panel_normal, near_block=near_block, far_rows=far_rows, far_basis=far_basis, block_ranks=block_ranks)


time_step = 0.1
softening = 0.4


def along_first(field):
    return (field[:, 2:, 1:-1, 1:-1] - field[:, :-2, 1:-1, 1:-1]) * 0.5


def along_second(field):
    return (field[:, 1:-1, 2:, 1:-1] - field[:, 1:-1, :-2, 1:-1]) * 0.5


def along_third(field):
    return (field[:, 1:-1, 1:-1, 2:] - field[:, 1:-1, 1:-1, :-2]) * 0.5


def velocity_update(stress, velocity, material):
    accel_x = along_first(stress[0:1]) + along_second(stress[5:6]) + along_third(stress[4:5])
    accel_y = along_first(stress[5:6]) + along_second(stress[1:2]) + along_third(stress[3:4])
    accel_z = along_first(stress[4:5]) + along_second(stress[3:4]) + along_third(stress[2:3])
    acceleration = jnp.concatenate([accel_x, accel_y, accel_z], axis=0)
    return velocity + time_step * material[2:3] * acceleration


def stress_update(velocity, stress, material):
    speed_x = velocity[0:1]
    speed_y = velocity[1:2]
    speed_z = velocity[2:3]
    strain_xx = along_first(speed_x)
    strain_yy = along_second(speed_y)
    strain_zz = along_third(speed_z)
    strain_yz = 0.5 * (along_third(speed_y) + along_second(speed_z))
    strain_xz = 0.5 * (along_third(speed_x) + along_first(speed_z))
    strain_xy = 0.5 * (along_second(speed_x) + along_first(speed_y))
    lame_first = material[0:1]
    shear = material[1:2]
    soften = material[3:4]
    dilation = strain_xx + strain_yy + strain_zz
    isotropic = (lame_first + (2.0 / 3.0) * shear) * dilation
    change_xx = isotropic + soften * (lame_first * dilation + 2.0 * shear * strain_xx - isotropic)
    change_yy = isotropic + soften * (lame_first * dilation + 2.0 * shear * strain_yy - isotropic)
    change_zz = isotropic + soften * (lame_first * dilation + 2.0 * shear * strain_zz - isotropic)
    change_yz = soften * 2.0 * shear * strain_yz
    change_xz = soften * 2.0 * shear * strain_xz
    change_xy = soften * 2.0 * shear * strain_xy
    change = jnp.concatenate([change_xx, change_yy, change_zz, change_yz, change_xz, change_xy], axis=0)
    return stress + time_step * change


def pad_rim(field):
    return jnp.pad(field, ((0, 0), (1, 1), (1, 1), (1, 1)))


def tractions_of(picked, normal):
    first = picked[0] * normal[0] + picked[5] * normal[1] + picked[4] * normal[2]
    second = picked[5] * normal[0] + picked[1] * normal[1] + picked[3] * normal[2]
    third = picked[4] * normal[0] + picked[3] * normal[1] + picked[2] * normal[2]
    return jnp.stack([first, second, third], axis=0)


def reference(stress_in, velocity_in, lame_lambda, shear_modulus, buoyancy, yield_flags, panel_cell, panel_normal, near_block, far_rows, far_basis, block_ranks):
    soften = jnp.where(yield_flags == 1, softening, 1.0).astype(jnp.float32)
    material = jnp.stack([lame_lambda, shear_modulus, buoyancy, soften], axis=0)
    stress = stress_in
    velocity = velocity_in
    for substep in range(SUB):
        velocity = velocity_update(pad_rim(stress), velocity, material)
        stress = stress_update(pad_rim(velocity), stress, material)
    blocks_all = N_GX * N_GY * N_GZ
    owner = jnp.arange(PANELS, dtype=jnp.int32) // PAN_DEV
    owner_x = owner // (N_GY * N_GZ)
    owner_y = (owner // N_GZ) % N_GY
    owner_z = owner % N_GZ
    local_x = panel_cell // (CY * CZ)
    local_y = (panel_cell // CZ) % CY
    local_z = panel_cell % CZ
    picked = stress_in[:, owner_x * CX + local_x, owner_y * CY + local_y, owner_z * CZ + local_z]
    traction = tractions_of(picked, panel_normal)
    cluster_size = PANELS // CLUST
    basis = far_basis.reshape(blocks_all, RANK, CLUST, cluster_size)
    grouped = traction.reshape(3, CLUST, cluster_size)
    projected = jnp.einsum('drcp,kcp->dcrk', basis, grouped, precision=lax.Precision.HIGHEST)
    rank_mask = (jnp.arange(RANK, dtype=jnp.int32)[None, None, :] < block_ranks[:, :, None]).astype(jnp.float32)
    projected = (projected * rank_mask[:, :, :, None]).reshape(blocks_all, CLUST * RANK, 3)
    row_factors = far_rows.reshape(blocks_all, PAN_DEV, CLUST * RANK)
    far_term = jnp.einsum('dpj,djk->kdp', row_factors, projected, precision=lax.Precision.HIGHEST)
    owned = traction.reshape(3, blocks_all, PAN_DEV)
    near_term = jnp.einsum('dpq,kdq->kdp', near_block.reshape(blocks_all, PAN_DEV, PAN_DEV), owned, precision=lax.Precision.HIGHEST)
    displacement = (near_term + far_term).reshape(3, PANELS)
    return stress, velocity, displacement
```

```python
import jax
import jax.numpy as jnp
from jax import lax
from jax.sharding import PartitionSpec as P

SUB = 2
RANK = 8
CLUST = 32
GX = ("x", "yl", "c")
ALL = GX + ("gy", "gz")


time_step = 0.1
softening = 0.4


def padded_2(x, sides, width):
    for axis, dim in sides:
        peers, length = (lax.axis_size(axis), x.shape[dim])
        up = [(i, (i + 1) % peers) for i in range(peers - 1)]
        down = [(j, i) for i, j in up]
        last = lax.slice_in_dim(x, length - width, length, axis=dim)
        first = lax.slice_in_dim(x, 0, width, axis=dim)
        before = lax.ppermute(last, axis, up)
        after = lax.ppermute(first, axis, down)
        x = jnp.concatenate([before, x, after], axis=dim)
    return x


def along_first(field):
    return (field[:, 2:, 1:-1, 1:-1] - field[:, :-2, 1:-1, 1:-1]) * 0.5


def along_second(field):
    return (field[:, 1:-1, 2:, 1:-1] - field[:, 1:-1, :-2, 1:-1]) * 0.5


def along_third(field):
    return (field[:, 1:-1, 1:-1, 2:] - field[:, 1:-1, 1:-1, :-2]) * 0.5


def velocity_update(stress, velocity, material):
    accel_x = along_first(stress[0:1]) + along_second(stress[5:6]) + along_third(stress[4:5])
    accel_y = along_first(stress[5:6]) + along_second(stress[1:2]) + along_third(stress[3:4])
    accel_z = along_first(stress[4:5]) + along_second(stress[3:4]) + along_third(stress[2:3])
    acceleration = jnp.concatenate([accel_x, accel_y, accel_z], axis=0)
    return velocity + time_step * material[2:3] * acceleration


def stress_update(velocity, stress, material):
    speed_x = velocity[0:1]
    speed_y = velocity[1:2]
    speed_z = velocity[2:3]
    strain_xx = along_first(speed_x)
    strain_yy = along_second(speed_y)
    strain_zz = along_third(speed_z)
    strain_yz = 0.5 * (along_third(speed_y) + along_second(speed_z))
    strain_xz = 0.5 * (along_third(speed_x) + along_first(speed_z))
    strain_xy = 0.5 * (along_second(speed_x) + along_first(speed_y))
    lame_first = material[0:1]
    shear = material[1:2]
    soften = material[3:4]
    dilation = strain_xx + strain_yy + strain_zz
    isotropic = (lame_first + 2.0 / 3.0 * shear) * dilation
    change_xx = isotropic + soften * (lame_first * dilation + 2.0 * shear * strain_xx - isotropic)
    change_yy = isotropic + soften * (lame_first * dilation + 2.0 * shear * strain_yy - isotropic)
    change_zz = isotropic + soften * (lame_first * dilation + 2.0 * shear * strain_zz - isotropic)
    change_yz = soften * 2.0 * shear * strain_yz
    change_xz = soften * 2.0 * shear * strain_xz
    change_xy = soften * 2.0 * shear * strain_xy
    change = jnp.concatenate(
        [change_xx, change_yy, change_zz, change_yz, change_xz, change_xy], axis=0
    )
    return stress + time_step * change


def tractions_of(picked, normal):
    first = picked[0] * normal[0] + picked[5] * normal[1] + picked[4] * normal[2]
    second = picked[5] * normal[0] + picked[1] * normal[1] + picked[3] * normal[2]
    third = picked[4] * normal[0] + picked[3] * normal[1] + picked[2] * normal[2]
    return jnp.stack([first, second, third], axis=0)


def spread(x, axes):
    peers = lax.axis_size(axes)
    return lax.all_to_all(jnp.broadcast_to(x[None], (peers,) + x.shape), axes, 0, 0)


def gathered(traction):
    block = spread(traction, "gz")
    block = spread(block, ("gy", "yl"))
    block = spread(block, "x")
    other = lax.ppermute(block, "c", [(0, 1), (1, 0)])
    mine = lax.axis_index("c") == 0
    both = jnp.stack([jnp.where(mine, block, other), jnp.where(mine, other, block)], axis=0)
    c, x, y, z, k, q = both.shape
    yl = lax.axis_size("yl")
    both = both.reshape(c, x, y // yl, yl, z, k, q).transpose(5, 1, 3, 0, 2, 4, 6)
    return both.reshape(k, CLUST, -1)


def per_device(
    stress_in,
    velocity_in,
    lame_lambda,
    shear_modulus,
    buoyancy,
    yield_flags,
    panel_cell,
    panel_normal,
    near_block,
    far_rows,
    far_basis,
    block_ranks,
):
    soften = jnp.where(yield_flags == 1, softening, 1.0).astype(jnp.float32)
    material = jnp.stack([lame_lambda, shear_modulus, buoyancy, soften], axis=0)
    flattened = stress_in.reshape(6, -1)
    picked = jnp.take(flattened, panel_cell, axis=1)
    traction = tractions_of(picked, panel_normal)
    everything = gathered(traction)
    stress = stress_in
    velocity = velocity_in
    for substep in range(SUB):
        padded = padded_2(stress, ((GX, 1), ("gy", 2), ("gz", 3)), 1)
        velocity = velocity_update(padded, velocity, material)
        padded = padded_2(velocity, ((GX, 1), ("gy", 2), ("gz", 3)), 1)
        stress = stress_update(padded, stress, material)
    cluster_size = everything.shape[2]
    basis = far_basis.reshape(RANK, CLUST, cluster_size)
    grouped = everything
    projected = jnp.einsum("rcp,kcp->crk", basis, grouped, precision=lax.Precision.HIGHEST)
    rank_mask = (jnp.arange(RANK, dtype=jnp.int32)[None, :] < block_ranks[0][:, None]).astype(
        jnp.float32
    )
    projected = (projected * rank_mask[:, :, None]).reshape(CLUST * RANK, 3)
    far_term = jnp.einsum("pj,jk->kp", far_rows, projected, precision=lax.Precision.HIGHEST)
    near_term = jnp.einsum("pq,kq->kp", near_block, traction, precision=lax.Precision.HIGHEST)
    return (stress, velocity, near_term + far_term)


def solution(mesh):
    shape = dict(mesh.shape)
    fine = jax.sharding.Mesh(
        mesh.devices.reshape(shape["gx"] // 4, 2, 2, shape["gy"], shape["gz"]), ALL
    )
    zones = P(GX, "gy", "gz")
    fields = P(None, GX, "gy", "gz")
    return jax.shard_map(
        per_device,
        mesh=fine,
        in_specs=(
            fields,
            fields,
            zones,
            zones,
            zones,
            zones,
            P(ALL),
            P(None, ALL),
            P(ALL, None),
            P(ALL, None),
            P(ALL, None),
            P(ALL, None),
        ),
        out_specs=(fields, fields, P(None, ALL)),
        check_vma=False,
    )
```

```python
import jax
import jax.numpy as jnp
from jax import lax
from jax.experimental import pallas as pl
from jax.experimental.pallas import tpu as pltpu
from jax.sharding import PartitionSpec as P

RANK = 8
CLUST = 32
GX = ("x", "yl", "c")
ALL = GX + ("gy", "gz")
F32 = jnp.float32
HIGHEST = lax.Precision.HIGHEST

time_step = 0.1
softening = 0.4

FIELDS = 12
REACH = (4,) * 6 + (3,) * 4 + (2,) * 2
SIDE = 8
DEEP = 4
WIDE = SIDE + 2 * DEEP

X_TILES = [
    (f, d, yt) for f in range(FIELDS) for d in range(1, REACH[f] + 1) for yt in (0, 1) if d + yt <= REACH[f]
]
X_AT = {t: i for i, t in enumerate(X_TILES)}


def beyond(x):
    return max(-x, x - (SIDE - 1), 0)


Z_TILES = [
    (f, x, yt)
    for f in range(FIELDS)
    for x in range(-DEEP, SIDE + DEEP)
    for yt in (0, 1)
    if beyond(x) + yt + 1 <= REACH[f]
]
Z_AT = {t: i for i, t in enumerate(Z_TILES)}
Z_PACKED = -(-len(Z_TILES) // 16)


def lanes():
    return lax.broadcasted_iota(jnp.int32, (8, 128), 1)


def rows():
    return lax.broadcasted_iota(jnp.int32, (8, 128), 0)


def call(body, outs, n_in, scratch=(), name=None, flops=1000000, vmem=4 << 20):
    spec = pl.BlockSpec(memory_space=pltpu.VMEM)
    return pl.pallas_call(
        body,
        out_shape=[jax.ShapeDtypeStruct(s, F32) for s in outs],
        in_specs=[spec] * n_in,
        out_specs=[spec] * len(outs),
        scratch_shapes=list(scratch),
        cost_estimate=pl.CostEstimate(flops=flops, bytes_accessed=flops, transcendentals=0),
        compiler_params=pltpu.CompilerParams(vmem_limit_bytes=vmem),
        name=name,
    )


def own(stress, velocity, coefficients, f, x):
    if f < 6:
        return stress[f, x]
    if f < 9:
        return velocity[f - 6, x]
    return coefficients[f - 9, x]


def traction_body(stress, cell, normal, traction):
    z = jnp.broadcast_to(cell[...] % 128, (8, 128))
    row = jnp.broadcast_to(cell[...] // 128, (8, 128))
    here = [row == rows() + 8 * x for x in range(SIDE)]
    picked = []
    for f in range(6):
        total = jnp.zeros((8, 128), F32)
        for x in range(SIDE):
            at = jnp.take_along_axis(stress[f, x], z, axis=1, mode="promise_in_bounds")
            total = total + jnp.where(here[x], at, 0.0)
        picked.append(jnp.sum(total, axis=0, keepdims=True))
    n = [normal[k : k + 1, :] for k in range(3)]
    for k, (a, b, c) in enumerate(((0, 5, 4), (5, 1, 3), (4, 3, 2))):
        traction[k : k + 1, :] = picked[a] * n[0] + picked[b] * n[1] + picked[c] * n[2]


def sides_body(stress, velocity, lame, shear, buoyancy, flags, coefficients, up, down):
    for x in range(SIDE):
        soften = jnp.where(flags[x] == 1, softening, 1.0).astype(F32)
        mu = shear[x]
        coefficients[0, x] = (0.5 * time_step) * buoyancy[x]
        coefficients[1, x] = (0.5 * time_step) * (lame[x] + (1.0 - soften) * (2.0 / 3.0) * mu)
        coefficients[2, x] = time_step * soften * mu
    low = rows() < 4
    for f in range(FIELDS):
        for p in range(SIDE // 2):
            a = own(stress, velocity, coefficients, f, 2 * p)
            b = own(stress, velocity, coefficients, f, 2 * p + 1)
            i = f * (SIDE // 2) + p
            down[i] = jnp.where(low, a, pltpu.roll(b, 4, 0))
            up[i] = jnp.where(low, pltpu.roll(a, 4, 0), b)


def widen_y_body(stress, velocity, coefficients, from_low, from_high, beside, up, down):
    low = rows() < 4
    for f in range(FIELDS):
        for p in range(SIDE // 2):
            i = f * (SIDE // 2) + p
            a, b = from_high[i], from_low[i]
            beside[f, 2 * p] = jnp.where(low, a, pltpu.roll(b, 4, 0))
            beside[f, 2 * p + 1] = jnp.where(low, pltpu.roll(a, 4, 0), b)
    for i, (f, d, yt) in enumerate(X_TILES):
        for x, out in ((SIDE - d, up), (d - 1, down)):
            out[i] = beside[f, x] if yt else own(stress, velocity, coefficients, f, x)


def wide_tile(refs, f, x, yt):
    stress, velocity, coefficients, beside, x_low, x_high = refs
    if x < 0:
        return x_low[X_AT[f, -x, yt]]
    if x >= SIDE:
        return x_high[X_AT[f, x - (SIDE - 1), yt]]
    return beside[f, x] if yt else own(stress, velocity, coefficients, f, x)


def ends_body(stress, velocity, coefficients, beside, x_low, x_high, packed):
    refs = (stress, velocity, coefficients, beside, x_low, x_high)
    slot = lanes() // 8
    for t in range(Z_PACKED):
        total = None
        for k, (f, x, yt) in enumerate(Z_TILES[16 * t : 16 * t + 16]):
            turned = pltpu.roll(wide_tile(refs, f, x, yt), (4 + 8 * k) % 128, 1)
            total = turned if total is None else jnp.where(slot == k, turned, total)
        packed[t] = total


def step_body(
    stress, velocity, coefficients, beside, x_low, x_high, z_low, z_high, stress_out, velocity_out, held
):
    refs = (stress, velocity, coefficients, beside, x_low, x_high)
    first = lanes() % 8 < 4
    for f in range(FIELDS):
        for x in range(-DEEP, SIDE + DEEP):
            for yt in (0, 1):
                if beyond(x) + yt <= REACH[f]:
                    held[f, x + DEEP, 2 * yt] = wide_tile(refs, f, x, yt)
    for t in range(Z_PACKED):
        both = jnp.where(first, z_low[t], z_high[t])
        for k, (f, x, yt) in enumerate(Z_TILES[16 * t : 16 * t + 16]):
            held[f, x + DEEP, 2 * yt + 1] = pltpu.roll(both, (124 - 8 * k) % 128, 1)

    top, bottom = rows() == 7, rows() == 0
    right, left = lanes() == 127, lanes() == 0

    def ring(near, far, axis, size, last, start):
        nu, fu = pltpu.roll(near, size - 1, axis), pltpu.roll(far, size - 1, axis)
        nd, fd = pltpu.roll(near, 1, axis), pltpu.roll(far, 1, axis)
        return (
            jnp.where(last, fu, nu) - jnp.where(start, fd, nd),
            jnp.where(last, nu, fu) - jnp.where(start, nd, fd),
        )

    def along_x(f, i, tiles):
        return {t: held[f, i + 1, t] - held[f, i - 1, t] for t in tiles}

    def along_y(f, i, tiles):
        out = {}
        for zt in (0, 1):
            if zt in tiles or zt + 2 in tiles:
                out[zt], out[zt + 2] = ring(held[f, i, zt], held[f, i, zt + 2], 0, 8, top, bottom)
        return out

    def along_z(f, i, tiles):
        out = {}
        for yt in (0, 2):
            if yt in tiles or yt + 1 in tiles:
                out[yt], out[yt + 1] = ring(held[f, i, yt], held[f, i, yt + 1], 1, 128, right, left)
        return out

    def speed(i, tiles):
        for k, (a, b, c) in enumerate(((0, 5, 4), (5, 1, 3), (4, 3, 2))):
            dx, dy, dz = along_x(a, i, tiles), along_y(b, i, tiles), along_z(c, i, tiles)
            for t in tiles:
                held[6 + k, i, t] = held[6 + k, i, t] + held[9, i, t] * (dx[t] + dy[t] + dz[t])

    def strain(i, tiles, put):
        xx, yy, zz = along_x(6, i, tiles), along_y(7, i, tiles), along_z(8, i, tiles)
        for t in tiles:
            iso = held[10, i, t] * (xx[t] + yy[t] + zz[t])
            scale = held[11, i, t]
            for f, e in ((0, xx), (1, yy), (2, zz)):
                put(f, i, t, held[f, i, t] + (iso + scale * e[t]))
        for f, one, other in (
            (3, along_z(7, i, tiles), along_y(8, i, tiles)),
            (4, along_z(6, i, tiles), along_x(8, i, tiles)),
            (5, along_y(6, i, tiles), along_x(7, i, tiles)),
        ):
            for t in tiles:
                put(f, i, t, held[f, i, t] + 0.5 * held[11, i, t] * (one[t] + other[t]))

    def keep(f, i, t, value):
        held[f, i, t] = value

    def hand_out(f, i, t, value):
        stress_out[f, i - DEEP] = value

    everything = (0, 1, 2, 3)

    def loop(start, stop, body):
        def step(i, carry):
            body(i)
            return carry

        lax.fori_loop(start, stop, step, 0)

    loop(1, WIDE - 1, lambda i: speed(i, everything))
    loop(2, WIDE - 2, lambda i: strain(i, everything, keep))
    loop(3, WIDE - 3, lambda i: speed(i, (0, 1, 2)))

    def last(i):
        strain(i, (0,), hand_out)
        for k in range(3):
            velocity_out[k, i - DEEP] = held[6 + k, i, 0]

    loop(DEEP, DEEP + SIDE, last)


def panels_body(core, mine, other, traction, near, far, basis, ranks, out, sums):
    n_x, n_y, n_z = mine.shape[0], mine.shape[1], mine.shape[2] // 3
    per_core = n_y // 2 * n_z
    c = core[0]
    for which, source in ((c, mine), (1 - c, other)):
        def cluster(i, carry, which=which, source=source):
            x, yl, half = i // 4, i // 2 % 2, i % 2
            totals = [jnp.zeros((8, 128), F32) for _ in range(3)]
            for g in range(2):
                block = source[x, (half * 2 + g) * 2 + yl]
                start = ((x * 2 + yl) * 2 + which) * per_core + (half * 2 + g) * n_z
                for z in range(n_z):
                    part = basis[:, pl.ds(pl.multiple_of((start + z) * 128, 128), 128)]
                    for k in range(3):
                        totals[k] = totals[k] + part * block[3 * z + k : 3 * z + k + 1, :]
            at = ((x * 2 + yl) * 2 + which) * 2 + half
            for k in range(3):
                sums[k, pl.ds(pl.multiple_of(at * RANK, RANK), RANK), :] = totals[k]
            return carry

        lax.fori_loop(0, n_x * 4, cluster, 0)
    last = (((1,), (1,)), ((), ()))
    ones = jnp.ones((8, 128), F32)
    rank_of = lax.broadcasted_iota(jnp.int32, (CLUST, CLUST * RANK), 1)
    cluster_of = lax.broadcasted_iota(jnp.int32, (CLUST, CLUST * RANK), 0)
    spread_out = (rank_of // RANK == cluster_of).astype(F32)
    limit = jnp.dot(
        jnp.broadcast_to(ranks[...].astype(F32), (8, CLUST)), spread_out, preferred_element_type=F32
    )
    rank = lax.broadcasted_iota(jnp.int32, (8, CLUST * RANK), 1) % RANK
    kept = rank.astype(F32) + 0.5 < limit
    row = lax.broadcasted_iota(jnp.int32, (8, CLUST * RANK), 0)
    projected = jnp.zeros((8, CLUST * RANK), F32)
    for k in range(3):
        total = lax.dot_general(ones, sums[k], last, precision=HIGHEST, preferred_element_type=F32)
        projected = jnp.where(kept & (row == k), total, projected)
    far_term = lax.dot_general(projected, far[...], last, precision=HIGHEST, preferred_element_type=F32)
    near_term = lax.dot_general(traction[...], near[...], last, precision=HIGHEST, preferred_element_type=F32)
    out[...] = near_term + far_term[0:3, :]


def both_ways(up, down, axis):
    peers = lax.axis_size(axis)
    rising = [(i, i + 1) for i in range(peers - 1)]
    falling = [(j, i) for i, j in rising]
    return lax.ppermute(up, axis, rising), lax.ppermute(down, axis, falling)


def spread(x, axes):
    peers = lax.axis_size(axes)
    return lax.all_to_all(jnp.broadcast_to(x[None], (peers,) + x.shape), axes, 0, 0)


def after(x, *others):
    return lax.optimization_barrier((x,) + others)[0]


def per_device(
    stress,
    velocity,
    lame_lambda,
    shear_modulus,
    buoyancy,
    yield_flags,
    panel_cell,
    panel_normal,
    near_block,
    far_rows,
    far_basis,
    block_ranks,
):
    tile = (SIDE, 128)
    (traction,) = call(traction_body, [(3, 128)], 3, name="traction")(
        stress, panel_cell.reshape(1, 128), panel_normal
    )
    half = (FIELDS * SIDE // 2,) + tile
    coefficients, up, down = call(sides_body, [(3, SIDE) + tile, half, half], 6, name="sides")(
        stress, velocity, lame_lambda, shear_modulus, buoyancy, yield_flags
    )
    y_low, y_high = both_ways(up, down, "gy")
    block = spread(after(traction, up, down), "gz")
    x_message = (len(X_TILES),) + tile
    beside, up, down = call(
        widen_y_body, [(FIELDS, SIDE) + tile, x_message, x_message], 5, name="widen_y"
    )(stress, velocity, coefficients, y_low, y_high)
    x_low, x_high = both_ways(up, down, GX)
    block = spread(after(block.reshape(-1, 128), up, down), ("gy", "yl"))
    (packed,) = call(ends_body, [(Z_PACKED,) + tile], 6, name="ends")(
        stress, velocity, coefficients, beside, x_low, x_high
    )
    z_low, z_high = both_ways(packed, packed, "gz")
    block = spread(after(block, packed), "x")
    other = lax.ppermute(block, "c", [(0, 1), (1, 0)])
    stress_out, velocity_out = call(
        step_body,
        [stress.shape, velocity.shape],
        8,
        scratch=[pltpu.VMEM((FIELDS, WIDE, 4) + tile, F32)],
        name="step",
        flops=20000000,
        vmem=8 << 20,
    )(stress, velocity, coefficients, beside, x_low, x_high, z_low, z_high)
    displacement = panels(block, other, traction, near_block, far_rows, far_basis, block_ranks, lax.axis_index("c"))
    return stress_out, velocity_out, displacement


def panels(block, other, traction, near_block, far_rows, far_basis, block_ranks, core):
    spec = pl.BlockSpec(memory_space=pltpu.VMEM)
    return pl.pallas_call(
        panels_body,
        out_shape=jax.ShapeDtypeStruct((3, 128), F32),
        in_specs=[pl.BlockSpec(memory_space=pltpu.SMEM)] + [spec] * 7,
        out_specs=spec,
        scratch_shapes=[pltpu.VMEM((3, CLUST * RANK, 128), F32)],
        cost_estimate=pl.CostEstimate(flops=3000000, bytes_accessed=3000000, transcendentals=0),
        compiler_params=pltpu.CompilerParams(vmem_limit_bytes=8 << 20),
        name="panels",
    )(core.astype(jnp.int32).reshape(1), block, other, traction, near_block, far_rows, far_basis, block_ranks)


def solution(mesh):
    shape = dict(mesh.shape)
    fine = jax.sharding.Mesh(
        mesh.devices.reshape(shape["gx"] // 4, 2, 2, shape["gy"], shape["gz"]), ALL
    )
    zones = P(GX, "gy", "gz")
    fields = P(None, GX, "gy", "gz")
    return jax.shard_map(
        per_device,
        mesh=fine,
        in_specs=(
            fields,
            fields,
            zones,
            zones,
            zones,
            zones,
            P(ALL),
            P(None, ALL),
            P(ALL, None),
            P(ALL, None),
            P(ALL, None),
            P(ALL, None),
        ),
        out_specs=(fields, fields, P(None, ALL)),
        check_vma=False,
    )
```

```python
import jax
import jax.numpy as jnp
from jax import lax
from jax.experimental import pallas as pl
from jax.experimental.pallas import tpu as pltpu
from jax.sharding import PartitionSpec as P

RANK = 8
CLUST = 32
GX = ("x", "yl", "c")
ALL = GX + ("gy", "gz")
F32 = jnp.float32
HIGHEST = lax.Precision.HIGHEST

FIRST = 56 << 20
time_step = 0.1
softening = 0.4

FIELDS = 12
REACH = (4,) * 6 + (3,) * 4 + (2,) * 2
SIDE = 8
DEEP = 4
WIDE = SIDE + 2 * DEEP

X_TILES = [
    (f, d, yt) for f in range(FIELDS) for d in range(1, REACH[f] + 1) for yt in (0, 1) if d + yt <= REACH[f]
]
X_AT = {t: i for i, t in enumerate(X_TILES)}


def beyond(x):
    return max(-x, x - (SIDE - 1), 0)


Z_TILES = [
    (f, x, yt)
    for f in range(FIELDS)
    for x in range(-DEEP, SIDE + DEEP)
    for yt in (0, 1)
    if beyond(x) + yt + 1 <= REACH[f]
]
Z_AT = {t: i for i, t in enumerate(Z_TILES)}
Z_PACKED = -(-len(Z_TILES) // 16)


def lanes():
    return lax.broadcasted_iota(jnp.int32, (8, 128), 1)


def rows():
    return lax.broadcasted_iota(jnp.int32, (8, 128), 0)


def call(body, outs, specs, scratch=(), name=None, flops=1000000, vmem=4 << 20, in_place=None):
    spec = pl.BlockSpec(memory_space=pltpu.VMEM)
    return pl.pallas_call(
        body,
        out_shape=[s if hasattr(s, "dtype") else jax.ShapeDtypeStruct(s, F32) for s in outs],
        in_specs=[pl.BlockSpec(memory_space=m) for m in specs],
        out_specs=[spec] * len(outs),
        scratch_shapes=list(scratch),
        cost_estimate=pl.CostEstimate(flops=flops, bytes_accessed=flops, transcendentals=0),
        compiler_params=pltpu.CompilerParams(vmem_limit_bytes=vmem),
        input_output_aliases=in_place or {},
        name=name,
    )


def odd(axis):
    return lax.axis_index(axis) % 2


def swapped(parity, a, b):
    return jnp.where(parity == 0, a, b), jnp.where(parity == 0, b, a)


def first_body(
    stress, velocity, lame, shear, buoyancy, flags, cell, normal, near, far, ranks,
    fields, traction, one, two, near_out, far_out, ranks_out,
    lame_in, shear_in, buoyancy_in, flags_in, cell_in, normal_in, sems,
):
    copies = [
        pltpu.make_async_copy(source, target, sems.at[i])
        for i, (source, target) in enumerate(
            (
                (stress, fields.at[0:6]),
                (cell, cell_in),
                (normal, normal_in),
                (velocity, fields.at[6:9]),
                (lame, lame_in),
                (shear, shear_in),
                (buoyancy, buoyancy_in),
                (flags, flags_in),
                (near, near_out),
                (far, far_out),
                (ranks, ranks_out),
            )
        )
    ]
    for copy in copies:
        copy.start()
    for copy in copies[3:8]:
        copy.wait()
    for x in range(SIDE):
        soften = jnp.where(flags_in[x] == 1, softening, 1.0).astype(F32)
        mu = shear_in[x]
        fields[9, x] = (0.5 * time_step) * buoyancy_in[x]
        fields[10, x] = (0.5 * time_step) * (lame_in[x] + (1.0 - soften) * (2.0 / 3.0) * mu)
        fields[11, x] = time_step * soften * mu
    for copy in copies[:3]:
        copy.wait()
    z = jnp.broadcast_to(cell_in[...] % 128, (8, 128))
    row = jnp.broadcast_to(cell_in[...] // 128, (8, 128))
    here = [row == rows() + 8 * x for x in range(SIDE)]
    picked = []
    for f in range(6):
        total = jnp.zeros((8, 128), F32)
        for x in range(SIDE):
            at = jnp.take_along_axis(fields[f, x], z, axis=1, mode="promise_in_bounds")
            total = total + jnp.where(here[x], at, 0.0)
        picked.append(jnp.sum(total, axis=0, keepdims=True))
    n = [normal_in[k : k + 1, :] for k in range(3)]
    for k, (a, b, c) in enumerate(((0, 5, 4), (5, 1, 3), (4, 3, 2))):
        value = picked[a] * n[0] + picked[b] * n[1] + picked[c] * n[2]
        for peer in range(traction.shape[0]):
            traction[peer, k : k + 1, :] = value
    low = rows() < 4
    for f in range(FIELDS):
        for p in range(SIDE // 2):
            a, b = fields[f, 2 * p], fields[f, 2 * p + 1]
            i = f * (SIDE // 2) + p
            down = jnp.where(low, a, pltpu.roll(b, 4, 0))
            up = jnp.where(low, pltpu.roll(a, 4, 0), b)
            one[i], two[i] = swapped(odd("gy"), up, down)
    for copy in copies[8:]:
        copy.wait()


def widen_y_body(fields, from_one, from_two, block, beside, one, two, copies):
    low = rows() < 4
    for f in range(FIELDS):
        for p in range(SIDE // 2):
            i = f * (SIDE // 2) + p
            a, b = swapped(odd("gy"), from_one[i], from_two[i])
            beside[f, 2 * p] = jnp.where(low, a, pltpu.roll(b, 4, 0))
            beside[f, 2 * p + 1] = jnp.where(low, pltpu.roll(a, 4, 0), b)
    for i, (f, d, yt) in enumerate(X_TILES):
        source = beside if yt else fields
        one[i], two[i] = swapped(odd("c"), source[f, SIDE - d], source[f, d - 1])
    whole = jnp.concatenate([block[z] for z in range(block.shape[0])], axis=0)
    for peer in range(copies.shape[0]):
        copies[peer] = whole


def wide_tile(refs, f, x, yt):
    fields, beside, from_one, from_two = refs
    if beyond(x):
        i = X_AT[f, beyond(x), yt]
        return swapped(odd("c"), from_one[i], from_two[i])[x < 0]
    return beside[f, x] if yt else fields[f, x]


def ends_body(fields, beside, from_one, from_two, block, packed, wide, copies):
    refs = (fields, beside, from_one, from_two)
    for f in range(FIELDS):
        for x in range(-DEEP, SIDE + DEEP):
            for yt in (0, 1):
                if beyond(x) + yt <= REACH[f]:
                    wide[f, x + DEEP, yt] = wide_tile(refs, f, x, yt)
    slot = lanes() // 8
    for t in range(Z_PACKED):
        total = None
        for k, (f, x, yt) in enumerate(Z_TILES[16 * t : 16 * t + 16]):
            turned = pltpu.roll(wide[f, x + DEEP, yt], (4 + 8 * k) % 128, 1)
            total = turned if total is None else jnp.where(slot == k, turned, total)
        packed[t] = total
    for peer in range(copies.shape[0]):
        copies[peer] = block[...]


def step_body(
    start, from_one, from_two, mine, basis, wide, stress_out, velocity_out, own_sums, ends
):
    first = lanes() % 8 < 4
    for t in range(Z_PACKED):
        z_high, z_low = swapped(odd("gz"), from_one[t], from_two[t])
        both = jnp.where(first, z_low, z_high)
        for k, (f, x, yt) in enumerate(Z_TILES[16 * t : 16 * t + 16]):
            ends[f, x + DEEP, yt] = pltpu.roll(both, (124 - 8 * k) % 128, 1)

    def held(f, i, t):
        return (ends if t % 2 else wide).at[f, i, t // 2]

    top, bottom = rows() == 7, rows() == 0
    right, left = lanes() == 127, lanes() == 0

    def ring(near, far, axis, size, last, start):
        nu, fu = pltpu.roll(near, size - 1, axis), pltpu.roll(far, size - 1, axis)
        nd, fd = pltpu.roll(near, 1, axis), pltpu.roll(far, 1, axis)
        return (
            jnp.where(last, fu, nu) - jnp.where(start, fd, nd),
            jnp.where(last, nu, fu) - jnp.where(start, nd, fd),
        )

    def along_x(f, i, tiles):
        return {t: held(f, i + 1, t)[...] - held(f, i - 1, t)[...] for t in tiles}

    def along_y(f, i, tiles):
        out = {}
        for zt in (0, 1):
            if zt in tiles or zt + 2 in tiles:
                out[zt], out[zt + 2] = ring(held(f, i, zt)[...], held(f, i, zt + 2)[...], 0, 8, top, bottom)
        return out

    def along_z(f, i, tiles):
        out = {}
        for yt in (0, 2):
            if yt in tiles or yt + 1 in tiles:
                out[yt], out[yt + 1] = ring(held(f, i, yt)[...], held(f, i, yt + 1)[...], 1, 128, right, left)
        return out

    def speed(i, tiles):
        for k, (a, b, c) in enumerate(((0, 5, 4), (5, 1, 3), (4, 3, 2))):
            dx, dy, dz = along_x(a, i, tiles), along_y(b, i, tiles), along_z(c, i, tiles)
            for t in tiles:
                held(6 + k, i, t)[...] = held(6 + k, i, t)[...] + held(9, i, t)[...] * (dx[t] + dy[t] + dz[t])

    def strain(i, tiles, put):
        xx, yy, zz = along_x(6, i, tiles), along_y(7, i, tiles), along_z(8, i, tiles)
        for t in tiles:
            iso = held(10, i, t)[...] * (xx[t] + yy[t] + zz[t])
            scale = held(11, i, t)[...]
            for f, e in ((0, xx), (1, yy), (2, zz)):
                put(f, i, t, held(f, i, t)[...] + (iso + scale * e[t]))
        for f, one, other in (
            (3, along_z(7, i, tiles), along_y(8, i, tiles)),
            (4, along_z(6, i, tiles), along_x(8, i, tiles)),
            (5, along_y(6, i, tiles), along_x(7, i, tiles)),
        ):
            for t in tiles:
                put(f, i, t, held(f, i, t)[...] + 0.5 * held(11, i, t)[...] * (one[t] + other[t]))

    def keep(f, i, t, value):
        held(f, i, t)[...] = value

    def hand_out(f, i, t, value):
        stress_out[f, i - DEEP] = value

    everything = (0, 1, 2, 3)

    def loop(start, stop, body):
        def step(i, carry):
            body(i)
            return carry

        lax.fori_loop(start, stop, step, 0, unroll=2)

    def reaching(reach, body):
        for d in range(reach, 0, -1):
            tiles = tuple(t for t in everything if d + t // 2 + t % 2 <= reach)
            for i in (DEEP - d, DEEP + SIDE - 1 + d):
                body(i, tiles)
        tiles = tuple(t for t in everything if t // 2 + t % 2 <= reach)
        loop(DEEP, DEEP + SIDE, lambda i: body(i, tiles))

    reaching(3, speed)
    reaching(2, lambda i, tiles: strain(i, tiles, keep))
    reaching(1, speed)

    def last(i):
        strain(i, (0,), hand_out)
        for k in range(3):
            velocity_out[k, i - DEEP] = held(6 + k, i, 0)[...]

    loop(DEEP, DEEP + SIDE, last)

    def put(k, i, value):
        own_sums[k, pl.ds(pl.multiple_of(i * RANK, RANK), RANK), :] = value

    project(mine, odd("c"), basis, put)


def place_of(i, core):
    return (i // 2 * 2 + core) * 2 + i % 2


def project(source, core, basis, put):
    n_x, n_y, n_z = source.shape[0], source.shape[1], source.shape[2] // 3

    def cluster(i, carry):
        x, yl, half = i // 4, i // 2 % 2, i % 2
        totals = [jnp.zeros((8, 128), F32) for _ in range(3)]
        for g in range(2):
            block = source[x, (half * 2 + g) * 2 + yl]
            start = (place_of(i, core) * 2 + g) * n_z
            for z in range(n_z):
                part = basis[:, pl.ds(pl.multiple_of((start + z) * 128, 128), 128)]
                for k in range(3):
                    totals[k] = totals[k] + part * block[3 * z + k : 3 * z + k + 1, :]
        for k in range(3):
            put(k, i, totals[k])
        return carry

    lax.fori_loop(0, n_x * n_y // 2, cluster, 0)


def panels_body(other, own_sums, basis, ranks, traction, near, far, out, sums):
    def put(k, at, value):
        sums[k, pl.ds(pl.multiple_of(at * RANK, RANK), RANK), :] = value

    project(other, 1 - odd("c"), basis, lambda k, i, value: put(k, place_of(i, 1 - odd("c")), value))
    for i in range(own_sums.shape[1] // RANK):
        for k in range(3):
            put(k, place_of(i, odd("c")), own_sums[k, i * RANK : (i + 1) * RANK, :])
    last = (((1,), (1,)), ((), ()))
    ones = jnp.ones((8, 128), F32)
    rank_of = lax.broadcasted_iota(jnp.int32, (CLUST, CLUST * RANK), 1)
    cluster_of = lax.broadcasted_iota(jnp.int32, (CLUST, CLUST * RANK), 0)
    spread_out = (rank_of // RANK == cluster_of).astype(F32)
    limit = jnp.dot(
        jnp.broadcast_to(ranks[...].astype(F32), (8, CLUST)), spread_out, preferred_element_type=F32
    )
    rank = lax.broadcasted_iota(jnp.int32, (8, CLUST * RANK), 1) % RANK
    kept = rank.astype(F32) + 0.5 < limit
    row = lax.broadcasted_iota(jnp.int32, (8, CLUST * RANK), 0)
    projected = jnp.zeros((8, CLUST * RANK), F32)
    for k in range(3):
        total = lax.dot_general(ones, sums[k], last, precision=HIGHEST, preferred_element_type=F32)
        projected = jnp.where(kept & (row == k), total, projected)
    far_term = lax.dot_general(projected, far[...], last, precision=HIGHEST, preferred_element_type=F32)
    near_term = lax.dot_general(traction[0], near[...], last, precision=HIGHEST, preferred_element_type=F32)
    out[...] = near_term + far_term[0:3, :]


def both_ways(one, two, axis):
    peers = lax.axis_size(axis)
    pairs = [(i, i ^ 1) for i in range(peers)]
    others = [(i, i - 1 if i % 2 == 0 else i + 1) for i in range(1, peers - 1)]
    return lax.ppermute(one, axis, pairs), lax.ppermute(two, axis, others)


def spread(copies, axes):
    return lax.all_to_all(copies, axes, 0, 0)


def per_device(
    stress,
    velocity,
    lame_lambda,
    shear_modulus,
    buoyancy,
    yield_flags,
    panel_cell,
    panel_normal,
    near_block,
    far_rows,
    far_basis,
    block_ranks,
):
    tile = (SIDE, 128)
    zone = (SIDE,) + tile
    half = (FIELDS * SIDE // 2,) + tile
    x_message = (len(X_TILES),) + tile
    n_x, n_y, n_z = (lax.axis_size(a) for a in ("x", ("gy", "yl"), "gz"))
    traction_copies = (n_z, 3, 128)
    kept = [jax.ShapeDtypeStruct(a.shape, a.dtype) for a in (near_block, far_rows, block_ranks)]
    fields, block, one, two, near_block, far_rows, block_ranks = call(
        first_body,
        [(FIELDS,) + zone, traction_copies, half, half] + kept,
        [pltpu.HBM] * 11,
        scratch=[pltpu.VMEM(zone, F32)] * 3
        + [
            pltpu.VMEM(zone, jnp.int32),
            pltpu.VMEM((1, 128), jnp.int32),
            pltpu.VMEM((3, 128), F32),
            pltpu.SemaphoreType.DMA((11,)),
        ],
        name="first",
        vmem=FIRST,
    )(
        stress,
        velocity,
        lame_lambda,
        shear_modulus,
        buoyancy,
        yield_flags,
        panel_cell.reshape(1, 128),
        panel_normal,
        near_block,
        far_rows,
        block_ranks,
    )
    traction = block
    y_one, y_two = both_ways(one, two, "gy")
    block = spread(block, "gz")
    on_chip = pltpu.VMEM
    beside, one, two, block = call(
        widen_y_body,
        [(FIELDS,) + zone, x_message, x_message, (n_y, 3 * n_z, 128)],
        [on_chip] * 4,
        name="widen_y",
    )(fields, y_one, y_two, block)
    x_one, x_two = both_ways(one, two, GX)
    block = spread(block, ("gy", "yl"))
    wide_shape = (FIELDS, WIDE, 2) + tile
    packed, wide, block = call(
        ends_body,
        [(Z_PACKED,) + tile, wide_shape, (n_x, n_y, 3 * n_z, 128)],
        [on_chip] * 5,
        name="ends",
    )(fields, beside, x_one, x_two, block)
    z_one, z_two = both_ways(packed, packed, "gz")
    block = spread(block, "x")
    block, z_one, z_two = lax.optimization_barrier((block, z_one, z_two))
    other = lax.ppermute(block, "c", [(0, 1), (1, 0)])
    _, stress_out, velocity_out, own_sums = call(
        step_body,
        [wide_shape, stress.shape, velocity.shape, (3, CLUST // 2 * RANK, 128)],
        [on_chip] * 5,
        scratch=[pltpu.VMEM(wide_shape, F32)],
        in_place={0: 0},
        name="step",
        flops=20000000,
        vmem=8 << 20,
    )(wide, z_one, z_two, block, far_basis)
    displacement = panels(other, own_sums, far_basis, block_ranks, traction, near_block, far_rows)
    return stress_out, velocity_out, displacement


def panels(*operands):
    (out,) = call(
        panels_body,
        [(3, 128)],
        [pltpu.VMEM] * 7,
        scratch=[pltpu.VMEM((3, CLUST * RANK, 128), F32)],
        name="panels",
        flops=3000000,
        vmem=8 << 20,
    )(*operands)
    return out


def solution(mesh):
    shape = dict(mesh.shape)
    fine = jax.sharding.Mesh(
        mesh.devices.reshape(shape["gx"] // 4, 2, 2, shape["gy"], shape["gz"]), ALL
    )
    zones = P(GX, "gy", "gz")
    fields = P(None, GX, "gy", "gz")
    return jax.shard_map(
        per_device,
        mesh=fine,
        in_specs=(
            fields,
            fields,
            zones,
            zones,
            zones,
            zones,
            P(ALL),
            P(None, ALL),
            P(ALL, None),
            P(ALL, None),
            P(ALL, None),
            P(ALL, None),
        ),
        out_specs=(fields, fields, P(None, ALL)),
        check_vma=False,
    )
```

```python
import jax
import jax.numpy as jnp
from jax import lax
from jax.experimental import pallas as pl
from jax.experimental.pallas import tpu as pltpu
from jax.sharding import PartitionSpec as P

RANK = 8
CLUST = 32
GX = ("x", "yl", "c")
ALL = GX + ("gy", "gz")
F32 = jnp.float32
HIGHEST = lax.Precision.HIGHEST

FIRST = 56 << 20
time_step = 0.1
softening = 0.4

FIELDS = 12
REACH = (4,) * 6 + (3,) * 4 + (2,) * 2
SIDE = 8
DEEP = 4
WIDE = SIDE + 2 * DEEP

OF_X, OF_Y, OF_Z = (0, 5, 4), (5, 1, 3), (4, 3, 2)

Y_TILES = [(f, d) for f in range(FIELDS) for d in range(1, REACH[f] + 1) if d < DEEP or f in OF_Y]

X_TILES = [
    (f, d, yt)
    for f in range(FIELDS)
    for d in range(1, REACH[f] + 1)
    for yt in (0, 1)
    if d + yt < DEEP and d + yt <= REACH[f] or d + yt == DEEP and f in (OF_X + OF_Y if yt else OF_X)
]
X_AT = {t: i for i, t in enumerate(X_TILES)}


def beyond(x):
    return max(-x, x - (SIDE - 1), 0)


def known(f, x, yt):
    return (f, beyond(x), yt) in X_AT if beyond(x) else True


Z_TILES = [
    (f, x, yt)
    for f in range(FIELDS)
    for x in range(-DEEP, SIDE + DEEP)
    for yt in (0, 1)
    if beyond(x) + yt + 1 <= REACH[f] and known(f, x, yt)
]
Z_AT = {t: i for i, t in enumerate(Z_TILES)}
Z_PACKED = -(-len(Z_TILES) // 16)


def lanes():
    return lax.broadcasted_iota(jnp.int32, (8, 128), 1)


def rows():
    return lax.broadcasted_iota(jnp.int32, (8, 128), 0)


def call(body, outs, specs, scratch=(), name=None, flops=1000000, vmem=4 << 20, in_place=None):
    spec = pl.BlockSpec(memory_space=pltpu.VMEM)
    return pl.pallas_call(
        body,
        out_shape=[s if hasattr(s, "dtype") else jax.ShapeDtypeStruct(s, F32) for s in outs],
        in_specs=[pl.BlockSpec(memory_space=m) for m in specs],
        out_specs=[spec] * len(outs),
        scratch_shapes=list(scratch),
        cost_estimate=pl.CostEstimate(flops=flops, bytes_accessed=flops, transcendentals=0),
        compiler_params=pltpu.CompilerParams(vmem_limit_bytes=vmem),
        input_output_aliases=in_place or {},
        name=name,
    )


def odd(axis):
    return lax.axis_index(axis) % 2


def swapped(parity, a, b):
    return jnp.where(parity == 0, a, b), jnp.where(parity == 0, b, a)


def first_body(
    stress, velocity, lame, shear, buoyancy, flags, cell, normal, near, far, ranks,
    fields, traction, one, two, near_out, far_out, ranks_out,
    lame_in, shear_in, buoyancy_in, flags_in, cell_in, normal_in, sems,
):
    copies = [
        pltpu.make_async_copy(source, target, sems.at[i])
        for i, (source, target) in enumerate(
            (
                (stress, fields.at[0:6]),
                (cell, cell_in),
                (normal, normal_in),
                (velocity, fields.at[6:9]),
                (lame, lame_in),
                (shear, shear_in),
                (buoyancy, buoyancy_in),
                (flags, flags_in),
                (near, near_out),
                (far, far_out),
                (ranks, ranks_out),
            )
        )
    ]
    for copy in copies:
        copy.start()
    for copy in copies[3:8]:
        copy.wait()
    for x in range(SIDE):
        soften = jnp.where(flags_in[x] == 1, softening, 1.0).astype(F32)
        mu = shear_in[x]
        fields[9, x] = (0.5 * time_step) * buoyancy_in[x]
        fields[10, x] = (0.5 * time_step) * (lame_in[x] + (1.0 - soften) * (2.0 / 3.0) * mu)
        fields[11, x] = time_step * soften * mu
    for copy in copies[:3]:
        copy.wait()
    z = jnp.broadcast_to(cell_in[...] % 128, (8, 128))
    row = jnp.broadcast_to(cell_in[...] // 128, (8, 128))
    here = [row == rows() + 8 * x for x in range(SIDE)]
    picked = []
    for f in range(6):
        total = jnp.zeros((8, 128), F32)
        for x in range(SIDE):
            at = jnp.take_along_axis(fields[f, x], z, axis=1, mode="promise_in_bounds")
            total = total + jnp.where(here[x], at, 0.0)
        picked.append(jnp.sum(total, axis=0, keepdims=True))
    n = [normal_in[k : k + 1, :] for k in range(3)]
    for k, (a, b, c) in enumerate(zip(OF_X, OF_Y, OF_Z)):
        value = picked[a] * n[0] + picked[b] * n[1] + picked[c] * n[2]
        for peer in range(traction.shape[0]):
            traction[peer, k : k + 1, :] = value
    for i, (f, d) in enumerate(Y_TILES):
        one[i], two[i] = swapped(odd("gy"), fields[f, :, SIDE - d, :], fields[f, :, d - 1, :])
    for copy in copies[8:]:
        copy.wait()


def widen_y_body(fields, from_one, from_two, block, beside, one, two, copies):
    for i, (f, d) in enumerate(Y_TILES):
        high, low = swapped(odd("gy"), from_one[i], from_two[i])
        beside[f, :, d - 1, :] = high
        beside[f, :, SIDE - d, :] = low
    for i, (f, d, yt) in enumerate(X_TILES):
        source = beside if yt else fields
        one[i], two[i] = swapped(odd("c"), source[f, SIDE - d], source[f, d - 1])
    whole = jnp.concatenate([block[z] for z in range(block.shape[0])], axis=0)
    for peer in range(copies.shape[0]):
        copies[peer] = whole


def wide_tile(refs, f, x, yt):
    fields, beside, from_one, from_two = refs
    if beyond(x):
        i = X_AT[f, beyond(x), yt]
        return swapped(odd("c"), from_one[i], from_two[i])[x < 0]
    return beside[f, x] if yt else fields[f, x]


def ends_body(fields, beside, from_one, from_two, block, packed, wide, copies):
    refs = (fields, beside, from_one, from_two)
    for f in range(FIELDS):
        for x in range(-DEEP, SIDE + DEEP):
            for yt in (0, 1):
                if known(f, x, yt):
                    wide[f, x + DEEP, yt] = wide_tile(refs, f, x, yt)
    slot = lanes() // 8
    for t in range(Z_PACKED):
        total = None
        for k, (f, x, yt) in enumerate(Z_TILES[16 * t : 16 * t + 16]):
            turned = pltpu.roll(wide[f, x + DEEP, yt], (4 + 8 * k) % 128, 1)
            total = turned if total is None else jnp.where(slot == k, turned, total)
        packed[t] = total
    for peer in range(copies.shape[0]):
        copies[peer] = block[...]


def step_body(
    start, from_one, from_two, mine, basis, wide, stress_out, velocity_out, own_sums, ends
):
    first = lanes() % 8 < 4
    for t in range(Z_PACKED):
        z_high, z_low = swapped(odd("gz"), from_one[t], from_two[t])
        both = jnp.where(first, z_low, z_high)
        for k, (f, x, yt) in enumerate(Z_TILES[16 * t : 16 * t + 16]):
            ends[f, x + DEEP, yt] = pltpu.roll(both, (124 - 8 * k) % 128, 1)

    def held(f, i, t):
        return (ends if t % 2 else wide).at[f, i, t // 2]

    top, bottom = rows() == 7, rows() == 0
    right, left = lanes() == 127, lanes() == 0

    def ring(near, far, axis, size, last, start):
        nu, fu = pltpu.roll(near, size - 1, axis), pltpu.roll(far, size - 1, axis)
        nd, fd = pltpu.roll(near, 1, axis), pltpu.roll(far, 1, axis)
        return (
            jnp.where(last, fu, nu) - jnp.where(start, fd, nd),
            jnp.where(last, nu, fu) - jnp.where(start, nd, fd),
        )

    def along_x(f, i, tiles):
        return {t: held(f, i + 1, t)[...] - held(f, i - 1, t)[...] for t in tiles}

    def along_y(f, i, tiles):
        out = {}
        for zt in (0, 1):
            if zt in tiles or zt + 2 in tiles:
                out[zt], out[zt + 2] = ring(held(f, i, zt)[...], held(f, i, zt + 2)[...], 0, 8, top, bottom)
        return out

    def along_z(f, i, tiles):
        out = {}
        for yt in (0, 2):
            if yt in tiles or yt + 1 in tiles:
                out[yt], out[yt + 1] = ring(held(f, i, yt)[...], held(f, i, yt + 1)[...], 1, 128, right, left)
        return out

    def speed(i, tiles):
        for k, (a, b, c) in enumerate(zip(OF_X, OF_Y, OF_Z)):
            dx, dy, dz = along_x(a, i, tiles), along_y(b, i, tiles), along_z(c, i, tiles)
            for t in tiles:
                held(6 + k, i, t)[...] = held(6 + k, i, t)[...] + held(9, i, t)[...] * (dx[t] + dy[t] + dz[t])

    def strain(i, tiles, put):
        xx, yy, zz = along_x(6, i, tiles), along_y(7, i, tiles), along_z(8, i, tiles)
        for t in tiles:
            iso = held(10, i, t)[...] * (xx[t] + yy[t] + zz[t])
            scale = held(11, i, t)[...]
            for f, e in ((0, xx), (1, yy), (2, zz)):
                put(f, i, t, held(f, i, t)[...] + (iso + scale * e[t]))
        for f, one, other in (
            (3, along_z(7, i, tiles), along_y(8, i, tiles)),
            (4, along_z(6, i, tiles), along_x(8, i, tiles)),
            (5, along_y(6, i, tiles), along_x(7, i, tiles)),
        ):
            for t in tiles:
                put(f, i, t, held(f, i, t)[...] + 0.5 * held(11, i, t)[...] * (one[t] + other[t]))

    def keep(f, i, t, value):
        held(f, i, t)[...] = value

    def hand_out(f, i, t, value):
        stress_out[f, i - DEEP] = value

    everything = (0, 1, 2, 3)

    def loop(start, stop, body):
        def step(i, carry):
            body(i)
            return carry

        lax.fori_loop(start, stop, step, 0, unroll=8)

    def reaching(reach, body):
        for d in range(reach, 0, -1):
            tiles = tuple(t for t in everything if d + t // 2 + t % 2 <= reach)
            for i in (DEEP - d, DEEP + SIDE - 1 + d):
                body(i, tiles)
        tiles = tuple(t for t in everything if t // 2 + t % 2 <= reach)
        loop(DEEP, DEEP + SIDE, lambda i: body(i, tiles))

    reaching(3, speed)
    reaching(2, lambda i, tiles: strain(i, tiles, keep))
    reaching(1, speed)

    def last(i):
        strain(i, (0,), hand_out)
        for k in range(3):
            velocity_out[k, i - DEEP] = held(6 + k, i, 0)[...]

    loop(DEEP, DEEP + SIDE, last)

    def put(k, i, value):
        own_sums[k, pl.ds(pl.multiple_of(i * RANK, RANK), RANK), :] = value

    project(mine, odd("c"), basis, put)


def place_of(i, core):
    return (i // 2 * 2 + core) * 2 + i % 2


def project(source, core, basis, put):
    n_x, n_y, n_z = source.shape[0], source.shape[1], source.shape[2] // 3

    def cluster(i, carry):
        x, yl, half = i // 4, i // 2 % 2, i % 2
        totals = [jnp.zeros((8, 128), F32) for _ in range(3)]
        for g in range(2):
            block = source[x, (half * 2 + g) * 2 + yl]
            start = (place_of(i, core) * 2 + g) * n_z
            for z in range(n_z):
                part = basis[:, pl.ds(pl.multiple_of((start + z) * 128, 128), 128)]
                for k in range(3):
                    totals[k] = totals[k] + part * block[3 * z + k : 3 * z + k + 1, :]
        for k in range(3):
            put(k, i, totals[k])
        return carry

    lax.fori_loop(0, n_x * n_y // 2, cluster, 0, unroll=4)


def panels_body(other, own_sums, basis, ranks, traction, near, far, out, sums):
    def put(k, at, value):
        sums[k, pl.ds(pl.multiple_of(at * RANK, RANK), RANK), :] = value

    project(other, 1 - odd("c"), basis, lambda k, i, value: put(k, place_of(i, 1 - odd("c")), value))
    for i in range(own_sums.shape[1] // RANK):
        for k in range(3):
            put(k, place_of(i, odd("c")), own_sums[k, i * RANK : (i + 1) * RANK, :])
    last = (((1,), (1,)), ((), ()))
    ones = jnp.ones((8, 128), F32)
    rank_of = lax.broadcasted_iota(jnp.int32, (CLUST, CLUST * RANK), 1)
    cluster_of = lax.broadcasted_iota(jnp.int32, (CLUST, CLUST * RANK), 0)
    spread_out = (rank_of // RANK == cluster_of).astype(F32)
    limit = jnp.dot(
        jnp.broadcast_to(ranks[...].astype(F32), (8, CLUST)), spread_out, preferred_element_type=F32
    )
    rank = lax.broadcasted_iota(jnp.int32, (8, CLUST * RANK), 1) % RANK
    kept = rank.astype(F32) + 0.5 < limit
    row = lax.broadcasted_iota(jnp.int32, (8, CLUST * RANK), 0)
    projected = jnp.zeros((8, CLUST * RANK), F32)
    for k in range(3):
        total = lax.dot_general(ones, sums[k], last, precision=HIGHEST, preferred_element_type=F32)
        projected = jnp.where(kept & (row == k), total, projected)
    far_term = lax.dot_general(projected, far[...], last, precision=HIGHEST, preferred_element_type=F32)
    near_term = lax.dot_general(traction[0], near[...], last, precision=HIGHEST, preferred_element_type=F32)
    out[...] = near_term + far_term[0:3, :]


def both_ways(one, two, axis):
    peers = lax.axis_size(axis)
    pairs = [(i, i ^ 1) for i in range(peers)]
    others = [(i, i - 1 if i % 2 == 0 else i + 1) for i in range(1, peers - 1)]
    return lax.ppermute(one, axis, pairs), lax.ppermute(two, axis, others)


def spread(copies, axes):
    return lax.all_to_all(copies, axes, 0, 0)


def per_device(
    stress,
    velocity,
    lame_lambda,
    shear_modulus,
    buoyancy,
    yield_flags,
    panel_cell,
    panel_normal,
    near_block,
    far_rows,
    far_basis,
    block_ranks,
):
    tile = (SIDE, 128)
    zone = (SIDE,) + tile
    half = (len(Y_TILES),) + tile
    x_message = (len(X_TILES),) + tile
    n_x, n_y, n_z = (lax.axis_size(a) for a in ("x", ("gy", "yl"), "gz"))
    traction_copies = (n_z, 3, 128)
    kept = [jax.ShapeDtypeStruct(a.shape, a.dtype) for a in (near_block, far_rows, block_ranks)]
    fields, block, one, two, near_block, far_rows, block_ranks = call(
        first_body,
        [(FIELDS,) + zone, traction_copies, half, half] + kept,
        [pltpu.HBM] * 11,
        scratch=[pltpu.VMEM(zone, F32)] * 3
        + [
            pltpu.VMEM(zone, jnp.int32),
            pltpu.VMEM((1, 128), jnp.int32),
            pltpu.VMEM((3, 128), F32),
            pltpu.SemaphoreType.DMA((11,)),
        ],
        name="first",
        vmem=FIRST,
    )(
        stress,
        velocity,
        lame_lambda,
        shear_modulus,
        buoyancy,
        yield_flags,
        panel_cell.reshape(1, 128),
        panel_normal,
        near_block,
        far_rows,
        block_ranks,
    )
    traction = block
    y_one, y_two = both_ways(one, two, "gy")
    block = spread(block, "gz")
    on_chip = pltpu.VMEM
    beside, one, two, block = call(
        widen_y_body,
        [(FIELDS,) + zone, x_message, x_message, (n_y, 3 * n_z, 128)],
        [on_chip] * 4,
        name="widen_y",
    )(fields, y_one, y_two, block)
    x_one, x_two = both_ways(one, two, GX)
    block = spread(block, ("gy", "yl"))
    wide_shape = (FIELDS, WIDE, 2) + tile
    packed, wide, block = call(
        ends_body,
        [(Z_PACKED,) + tile, wide_shape, (n_x, n_y, 3 * n_z, 128)],
        [on_chip] * 5,
        name="ends",
    )(fields, beside, x_one, x_two, block)
    z_one, z_two = both_ways(packed, packed, "gz")
    block = spread(block, "x")
    block, z_one, z_two = lax.optimization_barrier((block, z_one, z_two))
    other = lax.ppermute(block, "c", [(0, 1), (1, 0)])
    _, stress_out, velocity_out, own_sums = call(
        step_body,
        [wide_shape, stress.shape, velocity.shape, (3, CLUST // 2 * RANK, 128)],
        [on_chip] * 5,
        scratch=[pltpu.VMEM(wide_shape, F32)],
        in_place={0: 0},
        name="step",
        flops=20000000,
        vmem=8 << 20,
    )(wide, z_one, z_two, block, far_basis)
    displacement = panels(other, own_sums, far_basis, block_ranks, traction, near_block, far_rows)
    return stress_out, velocity_out, displacement


def panels(*operands):
    (out,) = call(
        panels_body,
        [(3, 128)],
        [pltpu.VMEM] * 7,
        scratch=[pltpu.VMEM((3, CLUST * RANK, 128), F32)],
        name="panels",
        flops=3000000,
        vmem=8 << 20,
    )(*operands)
    return out


def solution(mesh):
    shape = dict(mesh.shape)
    fine = jax.sharding.Mesh(
        mesh.devices.reshape(shape["gx"] // 4, 2, 2, shape["gy"], shape["gz"]), ALL
    )
    zones = P(GX, "gy", "gz")
    fields = P(None, GX, "gy", "gz")
    return jax.shard_map(
        per_device,
        mesh=fine,
        in_specs=(
            fields,
            fields,
            zones,
            zones,
            zones,
            zones,
            P(ALL),
            P(None, ALL),
            P(ALL, None),
            P(ALL, None),
            P(ALL, None),
            P(ALL, None),
        ),
        out_specs=(fields, fields, P(None, ALL)),
        check_vma=False,
    )
```

```python
import jax
import jax.numpy as jnp
from jax import lax
from jax.experimental import pallas as pl
from jax.experimental.pallas import tpu as pltpu
from jax.sharding import PartitionSpec as P

RANK = 8
CLUST = 32
GX = ("x", "yl", "c")
ALL = GX + ("gy", "gz")
F32 = jnp.float32
HIGHEST = lax.Precision.HIGHEST

FIRST = 56 << 20
time_step = 0.1
softening = 0.4

FIELDS = 12
REACH = (4,) * 6 + (3,) * 4 + (2,) * 2
SIDE = 8
DEEP = 4
WIDE = SIDE + 2 * DEEP

OF_X, OF_Y, OF_Z = (0, 5, 4), (5, 1, 3), (4, 3, 2)

Y_TILES = [(f, d) for f in range(FIELDS) for d in range(1, REACH[f] + 1) if d < DEEP or f in OF_Y]

X_TILES = [
    (f, d, yt)
    for f in range(FIELDS)
    for d in range(1, REACH[f] + 1)
    for yt in (0, 1)
    if d + yt < DEEP and d + yt <= REACH[f] or d + yt == DEEP and f in (OF_X + OF_Y if yt else OF_X)
]
X_AT = {t: i for i, t in enumerate(X_TILES)}


def beyond(x):
    return max(-x, x - (SIDE - 1), 0)


def known(f, x, yt):
    return (f, beyond(x), yt) in X_AT if beyond(x) else True


Z_TILES = [
    (f, x, yt)
    for f in range(FIELDS)
    for x in range(-DEEP, SIDE + DEEP)
    for yt in (0, 1)
    if beyond(x) + yt + 1 <= REACH[f] and known(f, x, yt)
]
Z_AT = {t: i for i, t in enumerate(Z_TILES)}
Z_PACKED = -(-len(Z_TILES) // 16)


def lanes():
    return lax.broadcasted_iota(jnp.int32, (8, 128), 1)


def rows():
    return lax.broadcasted_iota(jnp.int32, (8, 128), 0)


def call(body, outs, specs, scratch=(), name=None, flops=1000000, vmem=4 << 20, in_place=None, away=()):
    spec = pl.BlockSpec(memory_space=pltpu.VMEM)
    return pl.pallas_call(
        body,
        out_shape=[s if hasattr(s, "dtype") else jax.ShapeDtypeStruct(s, F32) for s in outs],
        in_specs=[pl.BlockSpec(memory_space=m) for m in specs],
        out_specs=[pl.BlockSpec(memory_space=pltpu.HBM) if i in away else spec for i in range(len(outs))],
        scratch_shapes=list(scratch),
        cost_estimate=pl.CostEstimate(flops=flops, bytes_accessed=flops, transcendentals=0),
        compiler_params=pltpu.CompilerParams(vmem_limit_bytes=vmem),
        input_output_aliases=in_place or {},
        name=name,
    )


def odd(axis):
    return lax.axis_index(axis) % 2


def swapped(parity, a, b):
    return jnp.where(parity == 0, a, b), jnp.where(parity == 0, b, a)


def first_body(
    stress, velocity, lame, shear, buoyancy, flags, cell, normal, near, far, ranks,
    fields, traction, one, two, near_out, far_out, ranks_out,
    lame_in, shear_in, buoyancy_in, flags_in, cell_in, normal_in, sems,
):
    copies = [
        pltpu.make_async_copy(source, target, sems.at[i])
        for i, (source, target) in enumerate(
            (
                (stress, fields.at[0:6]),
                (cell, cell_in),
                (normal, normal_in),
                (velocity, fields.at[6:9]),
                (lame, lame_in),
                (shear, shear_in),
                (buoyancy, buoyancy_in),
                (flags, flags_in),
                (near, near_out),
                (far, far_out),
                (ranks, ranks_out),
            )
        )
    ]
    for copy in copies:
        copy.start()
    for copy in copies[3:8]:
        copy.wait()
    for x in range(SIDE):
        soften = jnp.where(flags_in[x] == 1, softening, 1.0).astype(F32)
        mu = shear_in[x]
        fields[9, x] = (0.5 * time_step) * buoyancy_in[x]
        fields[10, x] = (0.5 * time_step) * (lame_in[x] + (1.0 - soften) * (2.0 / 3.0) * mu)
        fields[11, x] = time_step * soften * mu
    for copy in copies[:3]:
        copy.wait()
    z = jnp.broadcast_to(cell_in[...] % 128, (8, 128))
    row = jnp.broadcast_to(cell_in[...] // 128, (8, 128))
    here = [row == rows() + 8 * x for x in range(SIDE)]
    picked = []
    for f in range(6):
        total = jnp.zeros((8, 128), F32)
        for x in range(SIDE):
            at = jnp.take_along_axis(fields[f, x], z, axis=1, mode="promise_in_bounds")
            total = total + jnp.where(here[x], at, 0.0)
        picked.append(jnp.sum(total, axis=0, keepdims=True))
    n = [normal_in[k : k + 1, :] for k in range(3)]
    for k, (a, b, c) in enumerate(zip(OF_X, OF_Y, OF_Z)):
        value = picked[a] * n[0] + picked[b] * n[1] + picked[c] * n[2]
        for peer in range(traction.shape[0]):
            traction[peer, k : k + 1, :] = value
    for i, (f, d) in enumerate(Y_TILES):
        one[i], two[i] = swapped(odd("gy"), fields[f, :, SIDE - d, :], fields[f, :, d - 1, :])
    for copy in copies[8:]:
        copy.wait()


def widen_y_body(fields, from_one, from_two, block, beside, one, two, copies):
    for i, (f, d) in enumerate(Y_TILES):
        high, low = swapped(odd("gy"), from_one[i], from_two[i])
        beside[f, :, d - 1, :] = high
        beside[f, :, SIDE - d, :] = low
    for i, (f, d, yt) in enumerate(X_TILES):
        source = beside if yt else fields
        one[i], two[i] = swapped(odd("c"), source[f, SIDE - d], source[f, d - 1])
    whole = jnp.concatenate([block[z] for z in range(block.shape[0])], axis=0)
    for peer in range(copies.shape[0]):
        copies[peer] = whole


def wide_tile(refs, f, x, yt):
    fields, beside, from_one, from_two = refs
    if beyond(x):
        i = X_AT[f, beyond(x), yt]
        return swapped(odd("c"), from_one[i], from_two[i])[x < 0]
    return beside[f, x] if yt else fields[f, x]


def ends_body(fields, beside, from_one, from_two, block, packed, wide, copies):
    refs = (fields, beside, from_one, from_two)
    for f in range(FIELDS):
        for x in range(-DEEP, SIDE + DEEP):
            for yt in (0, 1):
                if known(f, x, yt):
                    wide[f, x + DEEP, yt] = wide_tile(refs, f, x, yt)
    slot = lanes() // 8
    for t in range(Z_PACKED):
        total = None
        for k, (f, x, yt) in enumerate(Z_TILES[16 * t : 16 * t + 16]):
            turned = pltpu.roll(wide[f, x + DEEP, yt], (4 + 8 * k) % 128, 1)
            total = turned if total is None else jnp.where(slot == k, turned, total)
        packed[t] = total
    for peer in range(copies.shape[0]):
        copies[peer] = block[...]


def step_body(
    start, from_one, from_two, mine, basis,
    wide, stress_away, velocity_away, own_sums,
    ends, stress_out, velocity_out, sems,
):
    first = lanes() % 8 < 4
    for t in range(Z_PACKED):
        z_high, z_low = swapped(odd("gz"), from_one[t], from_two[t])
        both = jnp.where(first, z_low, z_high)
        for k, (f, x, yt) in enumerate(Z_TILES[16 * t : 16 * t + 16]):
            ends[f, x + DEEP, yt] = pltpu.roll(both, (124 - 8 * k) % 128, 1)

    def held(f, i, t):
        return (ends if t % 2 else wide).at[f, i, t // 2]

    top, bottom = rows() == 7, rows() == 0
    right, left = lanes() == 127, lanes() == 0

    def ring(near, far, axis, size, last, start):
        nu, fu = pltpu.roll(near, size - 1, axis), pltpu.roll(far, size - 1, axis)
        nd, fd = pltpu.roll(near, 1, axis), pltpu.roll(far, 1, axis)
        return (
            jnp.where(last, fu, nu) - jnp.where(start, fd, nd),
            jnp.where(last, nu, fu) - jnp.where(start, nd, fd),
        )

    def along_x(f, i, tiles):
        return {t: held(f, i + 1, t)[...] - held(f, i - 1, t)[...] for t in tiles}

    def along_y(f, i, tiles):
        out = {}
        for zt in (0, 1):
            if zt in tiles or zt + 2 in tiles:
                out[zt], out[zt + 2] = ring(held(f, i, zt)[...], held(f, i, zt + 2)[...], 0, 8, top, bottom)
        return out

    def along_z(f, i, tiles):
        out = {}
        for yt in (0, 2):
            if yt in tiles or yt + 1 in tiles:
                out[yt], out[yt + 1] = ring(held(f, i, yt)[...], held(f, i, yt + 1)[...], 1, 128, right, left)
        return out

    def speed(i, tiles):
        for k, (a, b, c) in enumerate(zip(OF_X, OF_Y, OF_Z)):
            dx, dy, dz = along_x(a, i, tiles), along_y(b, i, tiles), along_z(c, i, tiles)
            for t in tiles:
                held(6 + k, i, t)[...] = held(6 + k, i, t)[...] + held(9, i, t)[...] * (dx[t] + dy[t] + dz[t])

    def strain(i, tiles, put):
        xx, yy, zz = along_x(6, i, tiles), along_y(7, i, tiles), along_z(8, i, tiles)
        for t in tiles:
            iso = held(10, i, t)[...] * (xx[t] + yy[t] + zz[t])
            scale = held(11, i, t)[...]
            for f, e in ((0, xx), (1, yy), (2, zz)):
                put(f, i, t, held(f, i, t)[...] + (iso + scale * e[t]))
        for f, one, other in (
            (3, along_z(7, i, tiles), along_y(8, i, tiles)),
            (4, along_z(6, i, tiles), along_x(8, i, tiles)),
            (5, along_y(6, i, tiles), along_x(7, i, tiles)),
        ):
            for t in tiles:
                put(f, i, t, held(f, i, t)[...] + 0.5 * held(11, i, t)[...] * (one[t] + other[t]))

    def keep(f, i, t, value):
        held(f, i, t)[...] = value

    def hand_out(f, i, t, value):
        stress_out[f, i - DEEP] = value

    everything = (0, 1, 2, 3)

    def loop(start, stop, body):
        def step(i, carry):
            body(i)
            return carry

        lax.fori_loop(start, stop, step, 0, unroll=8)

    def reaching(reach, body):
        for d in range(reach, 0, -1):
            tiles = tuple(t for t in everything if d + t // 2 + t % 2 <= reach)
            for i in (DEEP - d, DEEP + SIDE - 1 + d):
                body(i, tiles)
        tiles = tuple(t for t in everything if t // 2 + t % 2 <= reach)
        loop(DEEP, DEEP + SIDE, lambda i: body(i, tiles))

    reaching(3, speed)
    reaching(2, lambda i, tiles: strain(i, tiles, keep))
    reaching(1, speed)

    def last(i):
        strain(i, (0,), hand_out)
        for k in range(3):
            velocity_out[k, i - DEEP] = held(6 + k, i, 0)[...]

    loop(DEEP, DEEP + SIDE, last)

    def put(k, i, value):
        own_sums[k, pl.ds(pl.multiple_of(i * RANK, RANK), RANK), :] = value

    stored = [
        pltpu.make_async_copy(stress_out, stress_away, sems.at[0]),
        pltpu.make_async_copy(velocity_out, velocity_away, sems.at[1]),
    ]
    for copy in stored:
        copy.start()
    project(mine, odd("c"), basis, put)
    for copy in stored:
        copy.wait()


def place_of(i, core):
    return (i // 2 * 2 + core) * 2 + i % 2


def project(source, core, basis, put):
    n_x, n_y, n_z = source.shape[0], source.shape[1], source.shape[2] // 3

    def cluster(i, carry):
        x, yl, half = i // 4, i // 2 % 2, i % 2
        totals = [jnp.zeros((8, 128), F32) for _ in range(3)]
        for g in range(2):
            block = source[x, (half * 2 + g) * 2 + yl]
            start = (place_of(i, core) * 2 + g) * n_z
            for z in range(n_z):
                part = basis[:, pl.ds(pl.multiple_of((start + z) * 128, 128), 128)]
                for k in range(3):
                    totals[k] = totals[k] + part * block[3 * z + k : 3 * z + k + 1, :]
        for k in range(3):
            put(k, i, totals[k])
        return carry

    lax.fori_loop(0, n_x * n_y // 2, cluster, 0, unroll=4)


def panels_body(other, own_sums, basis, ranks, traction, near, far, out, sums):
    def put(k, at, value):
        sums[k, pl.ds(pl.multiple_of(at * RANK, RANK), RANK), :] = value

    project(other, 1 - odd("c"), basis, lambda k, i, value: put(k, place_of(i, 1 - odd("c")), value))
    for i in range(own_sums.shape[1] // RANK):
        for k in range(3):
            put(k, place_of(i, odd("c")), own_sums[k, i * RANK : (i + 1) * RANK, :])
    last = (((1,), (1,)), ((), ()))
    ones = jnp.ones((8, 128), F32)
    rank_of = lax.broadcasted_iota(jnp.int32, (CLUST, CLUST * RANK), 1)
    cluster_of = lax.broadcasted_iota(jnp.int32, (CLUST, CLUST * RANK), 0)
    spread_out = (rank_of // RANK == cluster_of).astype(F32)
    limit = jnp.dot(
        jnp.broadcast_to(ranks[...].astype(F32), (8, CLUST)), spread_out, preferred_element_type=F32
    )
    rank = lax.broadcasted_iota(jnp.int32, (8, CLUST * RANK), 1) % RANK
    kept = rank.astype(F32) + 0.5 < limit
    row = lax.broadcasted_iota(jnp.int32, (8, CLUST * RANK), 0)
    projected = jnp.zeros((8, CLUST * RANK), F32)
    for k in range(3):
        total = lax.dot_general(ones, sums[k], last, precision=HIGHEST, preferred_element_type=F32)
        projected = jnp.where(kept & (row == k), total, projected)
    far_term = lax.dot_general(projected, far[...], last, precision=HIGHEST, preferred_element_type=F32)
    near_term = lax.dot_general(traction[0], near[...], last, precision=HIGHEST, preferred_element_type=F32)
    out[...] = near_term + far_term[0:3, :]


def both_ways(one, two, axis):
    peers = lax.axis_size(axis)
    pairs = [(i, i ^ 1) for i in range(peers)]
    others = [(i, i - 1 if i % 2 == 0 else i + 1) for i in range(1, peers - 1)]
    return lax.ppermute(one, axis, pairs), lax.ppermute(two, axis, others)


def spread(copies, axes):
    return lax.all_to_all(copies, axes, 0, 0)


def per_device(
    stress,
    velocity,
    lame_lambda,
    shear_modulus,
    buoyancy,
    yield_flags,
    panel_cell,
    panel_normal,
    near_block,
    far_rows,
    far_basis,
    block_ranks,
):
    tile = (SIDE, 128)
    zone = (SIDE,) + tile
    half = (len(Y_TILES),) + tile
    x_message = (len(X_TILES),) + tile
    n_x, n_y, n_z = (lax.axis_size(a) for a in ("x", ("gy", "yl"), "gz"))
    traction_copies = (n_z, 3, 128)
    kept = [jax.ShapeDtypeStruct(a.shape, a.dtype) for a in (near_block, far_rows, block_ranks)]
    fields, block, one, two, near_block, far_rows, block_ranks = call(
        first_body,
        [(FIELDS,) + zone, traction_copies, half, half] + kept,
        [pltpu.HBM] * 11,
        scratch=[pltpu.VMEM(zone, F32)] * 3
        + [
            pltpu.VMEM(zone, jnp.int32),
            pltpu.VMEM((1, 128), jnp.int32),
            pltpu.VMEM((3, 128), F32),
            pltpu.SemaphoreType.DMA((11,)),
        ],
        name="first",
        vmem=FIRST,
    )(
        stress,
        velocity,
        lame_lambda,
        shear_modulus,
        buoyancy,
        yield_flags,
        panel_cell.reshape(1, 128),
        panel_normal,
        near_block,
        far_rows,
        block_ranks,
    )
    traction = block
    y_one, y_two = both_ways(one, two, "gy")
    block = spread(block, "gz")
    on_chip = pltpu.VMEM
    beside, one, two, block = call(
        widen_y_body,
        [(FIELDS,) + zone, x_message, x_message, (n_y, 3 * n_z, 128)],
        [on_chip] * 4,
        name="widen_y",
    )(fields, y_one, y_two, block)
    x_one, x_two = both_ways(one, two, GX)
    block = spread(block, ("gy", "yl"))
    wide_shape = (FIELDS, WIDE, 2) + tile
    packed, wide, block = call(
        ends_body,
        [(Z_PACKED,) + tile, wide_shape, (n_x, n_y, 3 * n_z, 128)],
        [on_chip] * 5,
        name="ends",
    )(fields, beside, x_one, x_two, block)
    z_one, z_two = both_ways(packed, packed, "gz")
    block = spread(block, "x")
    block, z_one, z_two = lax.optimization_barrier((block, z_one, z_two))
    other = lax.ppermute(block, "c", [(0, 1), (1, 0)])
    _, stress_out, velocity_out, own_sums = call(
        step_body,
        [wide_shape, stress.shape, velocity.shape, (3, CLUST // 2 * RANK, 128)],
        [on_chip] * 5,
        scratch=[
            pltpu.VMEM(wide_shape, F32),
            pltpu.VMEM(stress.shape, F32),
            pltpu.VMEM(velocity.shape, F32),
            pltpu.SemaphoreType.DMA((2,)),
        ],
        in_place={0: 0},
        away=(1, 2),
        name="step",
        flops=20000000,
        vmem=8 << 20,
    )(wide, z_one, z_two, block, far_basis)
    displacement = panels(other, own_sums, far_basis, block_ranks, traction, near_block, far_rows)
    return stress_out, velocity_out, displacement


def panels(*operands):
    (out,) = call(
        panels_body,
        [(3, 128)],
        [pltpu.VMEM] * 7,
        scratch=[pltpu.VMEM((3, CLUST * RANK, 128), F32)],
        name="panels",
        flops=3000000,
        vmem=8 << 20,
    )(*operands)
    return out


def solution(mesh):
    shape = dict(mesh.shape)
    fine = jax.sharding.Mesh(
        mesh.devices.reshape(shape["gx"] // 4, 2, 2, shape["gy"], shape["gz"]), ALL
    )
    zones = P(GX, "gy", "gz")
    fields = P(None, GX, "gy", "gz")
    return jax.shard_map(
        per_device,
        mesh=fine,
        in_specs=(
            fields,
            fields,
            zones,
            zones,
            zones,
            zones,
            P(ALL),
            P(None, ALL),
            P(ALL, None),
            P(ALL, None),
            P(ALL, None),
            P(ALL, None),
        ),
        out_specs=(fields, fields, P(None, ALL)),
        check_vma=False,
    )
```
